32 devices in a mesh: qubit: 16 (over z, x, core), head: 2 (over y).
Axes of the slice: x: 2, y: 2, z: 4, core: 2. Of those that a mesh axis runs over, the one named last changes fastest.
Arguments:
- tokens: bfloat16 [128, 256, 512], P('qubit'), may hold values from -6 to 6
- kv_cache: bfloat16 [128, 8, 384, 128], P('qubit', 'head'), may hold values from -6 to 6
- cache_age: int32 [128, 3], P('qubit'), may hold values from 1 to 8
- partner: int32 [128], P('qubit'), may hold values from 0 to 127, as said below
- slope: float32 [8], P('head'), may hold values from 0.03 to 1.5
- w_qkv: bfloat16 [3, 512, 512], P(None, None, 'head'), may hold values from -0.25 to 0.25
- w_o: bfloat16 [512, 512], replicated, may hold values from -0.25 to 0.25
- attn_gain: float32 [512], replicated, may hold values from 0.5 to 1.5
- mlp_gain: float32 [512], replicated, may hold values from 0.5 to 1.5
- w_in: bfloat16 [512, 2048], P(None, 'head'), may hold values from -0.25 to 0.25
- w_down: bfloat16 [2048, 512], P('head'), may hold values from -0.125 to 0.125
Outputs:
- decoded: bfloat16 [128, 256, 512], P('qubit', 'head')
The draws below stay inside these ranges and needn't reach their ends.
Inputs may be any that keep to these rules, and one draw needn't show every extreme that they name: partner pairs the qubits: partner[partner[q]] = q. With H = 8, the 8 qubits of device d (q // 8 = d) carry the colours 0 to 7, one each, in an order drawn per device; the qubit of colour c pairs with the qubit of colour c on device H + (d + c) mod H if d < H, on device (d - H - c) mod H if d >= H.
All inputs are finite; a program needn't handle non-finite values.
Results may differ from the reference program's by a relative error of at most 0.0065.
Values may be sent and summed in bfloat16 or wider, within the bound.
A program may use at most 128 MiB of HBM per device.

```python
import math
import jax
import jax.numpy as jnp
from jax import lax

D = 512
HEADS = 8
DH = 64
FF = 2048
STAB = 128
CACHE_R = 3
Q_DEV = 8
NEW = 256
KEYS = 384
QUBITS = 128


def draw_partner(key, part):
    devices = QUBITS // Q_DEV
    half_count = devices // 2
    second_key = jax.random.fold_in(key, 23)
    colors_row = jnp.arange(Q_DEV, dtype=jnp.int32)
    scores = jax.random.randint(second_key, (devices, Q_DEV), 0, 1 << 20) * Q_DEV + colors_row[None, :]
    order = jnp.argsort(scores, axis=1, stable=True).astype(jnp.int32)
    device_idx = jnp.arange(devices, dtype=jnp.int32)[:, None]
    lower_side = device_idx < half_count
    target_dev = jnp.where(lower_side, half_count + (device_idx + colors_row[None, :]) % half_count, (device_idx - half_count - colors_row[None, :]) % half_count)
    colors = colors_row[None, :]
    source = device_idx * Q_DEV + order
    target = target_dev * Q_DEV + order[target_dev, colors]
    return jnp.zeros((QUBITS,), jnp.int32).at[source.reshape(-1)].set(target.reshape(-1).astype(jnp.int32))


def with_ends(result, own_key, smallest, high):
    place = [jax.random.randint(jax.random.fold_in(own_key, axis), (), 0, length) for axis, length in enumerate(result.shape)]
    main_axis = result.shape.index(max(result.shape))
    beside = place[:main_axis] + [(place[main_axis] + 1) % result.shape[main_axis]] + place[main_axis + 1:]
    return result.at[tuple(place)].set(smallest).at[tuple(beside)].set(high)


def steps_of(own_key, dims, shards, smallest, high):
    level = 1.0
    for position, shards_of in shards:
        draws = jax.random.uniform(jax.random.fold_in(jax.random.fold_in(own_key, 6), position), (shards_of,), jnp.float32, smallest / len(shards), high / len(shards))
        level = level * jnp.repeat(jnp.exp(draws), dims[position] // shards_of).reshape((-1,) + (1,) * (len(dims) - 1 - position))
    return level


def scatter_about(key, shape, scale, most, split=(), held_as=jnp.bfloat16):
    array = scale * jax.random.normal(key, shape, jnp.float32)
    if split:
        array = array * steps_of(key, shape, split, -0.22, 0.18)
    return jnp.clip(array, -most, most).astype(held_as)


def setup_inputs(seed: int = 0) -> dict:
    streams_of = jax.random.split(jax.random.key(seed), 12)
    return {
        "tokens": scatter_about(streams_of[0], (QUBITS, NEW, D), 1.0, 6.0, ((0, 16),)),
        "kv_cache": scatter_about(streams_of[1], (QUBITS, HEADS, KEYS, 2 * DH), 1.0, 6.0, ((0, 16), (1, 2))),
        "cache_age": with_ends(jax.random.randint(streams_of[2], (QUBITS, CACHE_R), 1, 9), jax.random.fold_in(streams_of[2], 1), 1, 8).astype(jnp.int32),
        "partner": draw_partner(jax.random.fold_in(streams_of[11], 71), 0),
        "slope": jnp.clip(jnp.exp(math.log(1.5) - 3.912023 * jax.random.uniform(streams_of[4], (HEADS,), jnp.float32) ** steps_of(streams_of[4], (HEADS,), ((0, 2),), -0.2, 0.2)), 0.03, 1.5),
        "w_qkv": scatter_about(streams_of[5], (3, D, D), D ** -0.5, 0.25, ((2, 2),)),
        "w_o": scatter_about(streams_of[6], (D, D), D ** -0.5, 0.25),
        "attn_gain": jnp.clip(1.0 + 0.1 * jax.random.normal(streams_of[7], (D,), jnp.float32), 0.5, 1.5),
        "mlp_gain": jnp.clip(1.0 + 0.1 * jax.random.normal(streams_of[8], (D,), jnp.float32), 0.5, 1.5),
        "w_in": scatter_about(streams_of[9], (D, FF), D ** -0.5, 0.25, ((1, 2),)),
        "w_down": scatter_about(streams_of[10], (FF, D), FF ** -0.5, 0.125, ((0, 2),)),
    }


def rms_scale(values, gain):
    return values * lax.rsqrt(lax.optimization_barrier(jnp.mean(values * values, axis=-1, keepdims=True)) + 1e-06) * gain

def cache_bias(age_row, slope, new_len):
    key_age = jnp.repeat(age_row.astype(jnp.float32), STAB)
    query_round = (jnp.arange(new_len) // STAB).astype(jnp.float32)
    return -slope[:, None, None] * (key_age[None, None, :] + query_round[None, :, None])

def fresh_bias(slope, new_len):
    round_idx = jnp.arange(new_len) // STAB
    allowed = round_idx[None, :] <= round_idx[:, None]
    distance = (round_idx[:, None] - round_idx[None, :]).astype(jnp.float32)
    return jnp.where(allowed[None], -slope[:, None, None] * distance[None], -1e+30)

def reference(tokens, kv_cache, cache_age, partner, slope, w_qkv, w_o, attn_gain, mlp_gain, w_in, w_down):
    new_len = tokens.shape[1]
    scale = DH ** (-0.5)
    highest = lax.Precision.HIGHEST

    def one_qubit(index):
        widened = tokens[index].astype(jnp.float32)
        normed = rms_scale(widened, attn_gain).astype(jnp.bfloat16)
        queries = jnp.dot(normed, w_qkv[0], preferred_element_type=jnp.float32).astype(jnp.bfloat16).reshape(new_len, HEADS, DH)
        fresh_k = jnp.dot(normed, w_qkv[1], preferred_element_type=jnp.float32).astype(jnp.bfloat16).reshape(new_len, HEADS, DH)
        fresh_v = jnp.dot(normed, w_qkv[2], preferred_element_type=jnp.float32).astype(jnp.bfloat16).reshape(new_len, HEADS, DH)
        mate = partner[index]
        own_cache = kv_cache[index]
        mate_cache = kv_cache[mate]
        key_set = jnp.concatenate([own_cache[..., :DH], mate_cache[..., :DH], jnp.transpose(fresh_k, (1, 0, 2))], axis=1).astype(jnp.float32)
        value_set = jnp.concatenate([own_cache[..., DH:], mate_cache[..., DH:], jnp.transpose(fresh_v, (1, 0, 2))], axis=1).astype(jnp.float32)
        bias = jnp.concatenate([cache_bias(cache_age[index], slope, new_len), cache_bias(cache_age[mate], slope, new_len), fresh_bias(slope, new_len)], axis=2)
        logits = jnp.einsum('thd,hkd->htk', queries.astype(jnp.float32), key_set, precision=highest) * scale + bias
        top = lax.optimization_barrier(jnp.max(logits, axis=-1))
        weights = jnp.exp(logits - top[..., None])
        rounded = weights.astype(jnp.bfloat16).astype(jnp.float32)
        summed = jnp.einsum('htk,hkd->htd', rounded, value_set, precision=highest)
        attended = summed / lax.optimization_barrier(jnp.sum(weights, axis=-1))[..., None]
        attended = jnp.transpose(attended, (1, 0, 2)).reshape(new_len, HEADS * DH).astype(jnp.bfloat16)
        hidden_state = widened + jnp.dot(attended, w_o, preferred_element_type=jnp.float32)
        mlp_in = rms_scale(hidden_state, mlp_gain).astype(jnp.bfloat16)
        activated = jax.nn.gelu(jnp.dot(mlp_in, w_in, preferred_element_type=jnp.float32)).astype(jnp.bfloat16)
        return (hidden_state + jnp.dot(activated, w_down, preferred_element_type=jnp.float32)).astype(jnp.bfloat16)
    return lax.map(one_qubit, jnp.arange(QUBITS, dtype=jnp.int32))
```

```python
import functools

import jax
import jax.numpy as jnp
from jax import lax
from jax.experimental import pallas as pl
from jax.experimental.pallas import tpu as pltpu
from jax.sharding import PartitionSpec as P


DH = 64
STAB = 128
F32 = jnp.float32
BF16 = jnp.bfloat16

ANY_SPEC = pl.BlockSpec(memory_space=pl.ANY)
SMEM_SPEC = pl.BlockSpec(memory_space=pltpu.SMEM)


def whole(shape):
    zeros = (0,) * len(shape)
    return pl.BlockSpec(shape, lambda *_: zeros)


def mm(a, b):
    return jnp.dot(a, b, preferred_element_type=F32)


def rms(x, gain):
    return x * lax.rsqrt(jnp.mean(x * x, axis=-1, keepdims=True) + 1e-06) * gain


def cost(flops, nbytes, trans=0):
    return pl.CostEstimate(flops=flops, bytes_accessed=nbytes, transcendentals=trans)


def params():
    return pltpu.CompilerParams(vmem_limit_bytes=48 * 1024 * 1024)


def project_kernel(order_ref, x_ref, gain_ref, w_ref, after_ref, q_ref, k_ref, v_ref):
    normed = rms(x_ref[0].astype(F32), gain_ref[...]).astype(BF16)
    q_ref[...] = mm(normed, w_ref[0]).astype(BF16)
    k_ref[...] = mm(normed, w_ref[1]).astype(BF16)
    v_ref[...] = mm(normed, w_ref[2]).astype(BF16)


def head_attention(queries, parts):
    queries = queries * jnp.asarray(DH**-0.5, BF16)
    lane = lax.broadcasted_iota(jnp.int32, (1, queries.shape[0]), 1)
    blocks = []
    for keys, _, biases, firsts in parts:
        s = lax.dot_general(keys, queries, (((1,), (1,)), ((), ())), preferred_element_type=F32)
        for i, (bias, first) in enumerate(zip(biases, firsts)):
            block = s[i * STAB : (i + 1) * STAB] + bias
            if first:
                block = jnp.where(lane >= first, block, -1e30)
            blocks.append(block)
    top = blocks[0]
    for block in blocks[1:]:
        top = jnp.maximum(top, block)
    top = jnp.max(top, axis=0, keepdims=True)
    weights = [jnp.exp(block - top) for block in blocks]
    total = weights[0]
    for w in weights[1:]:
        total = total + w
    total = jnp.sum(total, axis=0, keepdims=True)
    at, summed = 0, None
    for _, values, biases, _ in parts:
        w = jnp.concatenate([x.astype(BF16) for x in weights[at : at + len(biases)]], axis=0)
        at += len(biases)
        term = lax.dot_general(values, w, (((0,), (0,)), ((), ())), preferred_element_type=F32)
        summed = term if summed is None else summed + term
    return summed / total, top + jnp.log(total)


def cache_part(cache_ref, head, age_ref, row, slope, rounds):
    kv = cache_ref[0, head]
    biases = [-slope * age_ref[row, r].astype(F32) for r in range(rounds)]
    return kv[:, :DH], kv[:, DH:], biases, [0] * rounds


def near_kernel(c, heads, rounds, new_rounds, order_ref, q_ref, k_ref, v_ref, cache_ref, age_ref, slope_ref, after_ref, o_ref):
    row = order_ref[c]
    hd = heads * DH
    for h in range(heads):
        cols = slice(h * DH, (h + 1) * DH)
        slope = slope_ref[h]
        fresh = (
            k_ref[:, cols],
            v_ref[:, cols],
            [slope * float(r) for r in range(new_rounds)],
            [r * STAB for r in range(new_rounds)],
        )
        out, lse = head_attention(q_ref[:, cols], [cache_part(cache_ref, h, age_ref, row, slope, rounds), fresh])
        o_ref[cols, :] = out
        o_ref[hd + h : hd + h + 1, :] = lse


def far_kernel(c, heads, rounds, order_ref, q_ref, cache_ref, age_ref, slope_ref, after_ref, o_ref, lse_scr):
    row = order_ref[c]
    hd = heads * DH
    lse_scr[...] = jnp.zeros_like(lse_scr)
    for h in range(heads):
        cols = slice(h * DH, (h + 1) * DH)
        out, lse = head_attention(q_ref[:, cols], [cache_part(cache_ref, h, age_ref, row, slope_ref[h], rounds)])
        o_ref[cols, :] = out.astype(BF16)
        hi = lse.astype(BF16).astype(F32)
        mid = (lse - hi).astype(BF16).astype(F32)
        lse_scr[h : h + 1, :] = hi
        lse_scr[heads + h : heads + h + 1, :] = mid
        lse_scr[2 * heads + h : 2 * heads + h + 1, :] = lse - hi - mid
    o_ref[hd:, :] = lse_scr[...].astype(BF16)


def join_kernel(heads, pos_ref, near_ref, far_ref, after_ref, *refs):
    outs, scr = refs[:-1], refs[-1]
    hd = heads * DH
    tail = far_ref[hd:, :].astype(F32)
    lse_far = tail[:heads] + tail[heads : 2 * heads] + tail[2 * heads : 3 * heads]
    lse_near = near_ref[hd : hd + heads, :]
    top = jnp.maximum(lse_near, lse_far)
    a, b = jnp.exp(lse_near - top), jnp.exp(lse_far - top)
    a, b = a / (a + b), b / (a + b)
    rows = []
    for h in range(heads):
        cols = slice(h * DH, (h + 1) * DH)
        rows.append(near_ref[cols, :] * a[h : h + 1] + far_ref[cols, :].astype(F32) * b[h : h + 1])
    scr[...] = jnp.transpose(jnp.concatenate(rows, axis=0))
    n, count = len(outs), outs[0].shape[0]
    for r, out in enumerate(outs):
        start = pl.multiple_of(lax.rem(pos_ref[0] + r, n) * count, count)
        out[...] = scr[pl.ds(start, count), :].astype(BF16)


def mlp_kernel(group, n, steps, order_ref, pos_ref, *refs):
    size = len(group)
    pieces = [refs[g * n : (g + 1) * n] for g in range(size)]
    xs = refs[size * n : size * (n + 1)]
    refs = refs[size * (n + 1) :]
    w_os, w_ins, w_downs, gain_ref = refs[:n], refs[n : 2 * n], refs[2 * n : 3 * n], refs[3 * n]
    out_ref, hid, acc, res, sems = refs[-5:]
    rows = pieces[0][0].shape[0]
    step = pl.program_id(0)

    @pl.when(step == 0)
    def _():
        for g in range(size):
            h = xs[g][0].astype(F32)
            for piece, w_o in zip(pieces[g], w_os):
                h += mm(piece[...], w_o[...])
            acc[g * rows : (g + 1) * rows] = h
            hid[g * rows : (g + 1) * rows] = rms(h, gain_ref[...]).astype(BF16)

    x = hid[...]
    total = acc[...]
    for w_in, w_dn in zip(w_ins, w_downs):
        total += mm(jax.nn.gelu(mm(x, w_in[...])).astype(BF16), w_dn[...])
    acc[...] = total

    @pl.when(step == steps - 1)
    def _():
        res[...] = acc[...].astype(BF16).reshape(res.shape)
        copies = [
            pltpu.make_async_copy(res.at[g], out_ref.at[order_ref[c]], sems.at[g]) for g, c in enumerate(group)
        ]
        for copy in copies:
            copy.start()
        for copy in copies:
            copy.wait()


def on_device(n_dev, n, tokens, kv_cache, cache_age, partner, slope, w_qkv, w_o, attn_gain, mlp_gain, w_in, w_down):
    count, new_len, width = tokens.shape
    heads, keys = kv_cache.shape[1], kv_cache.shape[2]
    hd = heads * DH
    rounds, new_rounds = keys // STAB, new_len // STAB
    half = n_dev // 2
    me = lax.axis_index("qubit").astype(jnp.int32)
    pos = lax.axis_index("head").astype(jnp.int32)
    owner = partner // count
    colour = jnp.where(me < half, (owner - me) % half, (me - half - owner) % half)
    slots = jnp.arange(count, dtype=jnp.int32)
    order = jnp.sum(jnp.where(colour[None, :] == slots[:, None], slots[None, :], 0), axis=1).astype(jnp.int32)
    pos1 = pos[None]
    gain1, gain2 = attn_gain[None], mlp_gain[None]
    perms = []
    for c in range(count):
        pairs = [(d, half + (d + c) % half) for d in range(half)]
        perms.append(pairs + [(b, a) for a, b in pairs])
    swaps = [[(a, (a + r) % n) for a in range(n)] for r in range(n)]
    sources = [(pos - r) % n for r in range(n)]
    w_os = [lax.dynamic_slice_in_dim(w_o, src * hd, hd, 0) for src in sources]

    w_ins, w_downs = [w_in], [w_down]
    for r in range(1, n):
        w_ins.append(lax.ppermute(w_in, "head", swaps[r]))
        w_downs.append(lax.ppermute(w_down, "head", swaps[r]))

    after = order
    qs, ks, vs, got_q = [], [], [], []
    one = jax.ShapeDtypeStruct((new_len, hd), BF16)
    for c in range(count):
        q, k, v = pl.pallas_call(
            project_kernel,
            grid_spec=pltpu.PrefetchScalarGridSpec(
                num_scalar_prefetch=1,
                grid=(1,),
                in_specs=[
                    pl.BlockSpec((1, new_len, width), lambda i, o, c=c: (o[c], 0, 0)),
                    whole((1, width)),
                    whole((3, width, hd)),
                    ANY_SPEC,
                ],
                out_specs=[whole((new_len, hd))] * 3,
            ),
            out_shape=[one] * 3,
            compiler_params=params(),
            cost_estimate=cost(6 * new_len * width * hd, 1500000),
        )(order, tokens, gain1, w_qkv, after)
        after = v
        got_q.append(lax.ppermute(q, "qubit", perms[c]))
        qs.append(q)
        ks.append(k)
        vs.append(v)

    near = []
    cache_spec = [pl.BlockSpec((1, heads, keys, 2 * DH), lambda i, o, c=c: (o[c], 0, 0, 0)) for c in range(count)]
    for c in range(count):
        after = pl.pallas_call(
            functools.partial(near_kernel, c, heads, rounds, new_rounds),
            grid_spec=pltpu.PrefetchScalarGridSpec(
                num_scalar_prefetch=1,
                grid=(1,),
                in_specs=[whole((new_len, hd))] * 3 + [cache_spec[c], SMEM_SPEC, SMEM_SPEC, ANY_SPEC],
                out_specs=whole((hd + 8, new_len)),
            ),
            out_shape=jax.ShapeDtypeStruct((hd + 8, new_len), F32),
            compiler_params=params(),
            cost_estimate=cost(4 * heads * new_len * 640 * DH * 4, 1000000),
        )(order, qs[c], ks[c], vs[c], kv_cache, cache_age, slope, after)
        near.append(after)

    back = []
    for c in range(count):
        after = pl.pallas_call(
            functools.partial(far_kernel, c, heads, rounds),
            grid_spec=pltpu.PrefetchScalarGridSpec(
                num_scalar_prefetch=1,
                grid=(1,),
                in_specs=[whole((new_len, hd)), cache_spec[c], SMEM_SPEC, SMEM_SPEC, ANY_SPEC],
                out_specs=whole((hd + 16, new_len)),
                scratch_shapes=[pltpu.VMEM((16, new_len), F32)],
            ),
            out_shape=jax.ShapeDtypeStruct((hd + 16, new_len), BF16),
            compiler_params=params(),
            cost_estimate=cost(4 * heads * new_len * 384 * DH * 4, 1000000),
        )(order, got_q[c], kv_cache, cache_age, slope, after)
        back.append(lax.ppermute(after, "qubit", perms[c]))

    pieces = [None] * count
    rows = new_len // n

    def join(c, after):
        parts = pl.pallas_call(
            functools.partial(join_kernel, heads),
            grid=(1,),
            in_specs=[SMEM_SPEC, whole((hd + 8, new_len)), whole((hd + 16, new_len)), ANY_SPEC],
            out_specs=[whole((rows, hd))] * n,
            out_shape=[jax.ShapeDtypeStruct((rows, hd), BF16)] * n,
            scratch_shapes=[pltpu.VMEM((new_len, hd), F32)],
            compiler_params=params(),
            cost_estimate=cost(1000000, 1000000),
        )(pos1, near[c], back[c], after)
        pieces[c] = [parts[0]] + [lax.ppermute(parts[r], "head", swaps[r]) for r in range(1, n)]
        return parts[0]

    ff = w_in.shape[1]
    steps = 2
    chunk = ff // steps
    out = None

    def mlp(group, out, after):
        size = len(group)
        x_specs = [pl.BlockSpec((1, rows, width), lambda i, o, p, c=c: (o[c], p[0], 0)) for c in group]
        ins = [part for c in group for part in pieces[c]] + [tokens] * size
        ins += w_os + w_ins + w_downs + [gain2, after]
        specs = [whole((rows, hd))] * (n * size) + x_specs + [whole((hd, width))] * n
        specs += [pl.BlockSpec((width, chunk), lambda i, o, p: (0, i))] * n
        specs += [pl.BlockSpec((chunk, width), lambda i, o, p: (i, 0))] * n + [whole((1, width)), ANY_SPEC]
        alias = {}
        if out is not None:
            alias = {len(ins) + 2: 0}
            ins.append(out)
            specs.append(ANY_SPEC)
        return pl.pallas_call(
            functools.partial(mlp_kernel, group, n, steps),
            grid_spec=pltpu.PrefetchScalarGridSpec(
                num_scalar_prefetch=2,
                grid=(steps,),
                in_specs=specs,
                out_specs=ANY_SPEC,
                scratch_shapes=[
                    pltpu.VMEM((size * rows, width), BF16),
                    pltpu.VMEM((size * rows, width), F32),
                    pltpu.VMEM((size, rows, width), BF16),
                    pltpu.SemaphoreType.DMA((size,)),
                ],
            ),
            out_shape=jax.ShapeDtypeStruct((count, rows, width), BF16),
            input_output_aliases=alias,
            compiler_params=params(),
            cost_estimate=cost(size * rows * width * (width + 2 * n * ff) * 2, 5000000),
        )(order, pos1, *ins)

    groups, start = [], 0
    while start < count:
        size = 2 if start < count - 2 else 1
        groups.append(tuple(range(start, min(start + size, count))))
        start += size
    ready = 0
    for group in groups:
        need = min(group[-1] + 2, count)
        while ready < need:
            after = join(ready, after)
            ready += 1
        out = mlp(group, out, after)
        after = out if group is groups[-1] else after
    return out


def solution(mesh):
    in_specs = (
        P("qubit", None, None),
        P("qubit", "head", None, None),
        P("qubit", None),
        P("qubit"),
        P("head"),
        P(None, None, "head"),
        P(),
        P(),
        P(),
        P(None, "head"),
        P("head", None),
    )
    return jax.shard_map(
        functools.partial(on_device, mesh.shape["qubit"], mesh.shape["head"]),
        mesh=mesh,
        in_specs=in_specs,
        out_specs=P("qubit", "head", None),
        check_vma=False,
    )
```

```python
import functools

import jax
import jax.numpy as jnp
from jax import lax
from jax.experimental import pallas as pl
from jax.experimental.pallas import tpu as pltpu
from jax.sharding import PartitionSpec as P


DH = 64
STAB = 128
F32 = jnp.float32
BF16 = jnp.bfloat16

PROJ = 4
GROUP = 2
VMEM_BYTES = 67043328
ANY_SPEC = pl.BlockSpec(memory_space=pl.ANY)
SMEM_SPEC = pl.BlockSpec(memory_space=pltpu.SMEM)


def whole(shape):
    zeros = (0,) * len(shape)
    return pl.BlockSpec(shape, lambda *_: zeros)


def mm(a, b):
    return jnp.dot(a, b, preferred_element_type=F32)


def rms(x, gain):
    return x * lax.rsqrt(jnp.mean(x * x, axis=-1, keepdims=True) + 1e-06) * gain


def cost(flops, nbytes, trans=0):
    return pl.CostEstimate(flops=flops, bytes_accessed=nbytes, transcendentals=trans)


def params():
    return pltpu.CompilerParams(vmem_limit_bytes=VMEM_BYTES)


def project_kernel(size, order_ref, x_ref, gain_ref, w_ref, after_ref, qkv_ref, *q_refs):
    step = pl.program_id(0)
    normed = rms(x_ref[0].astype(F32), gain_ref[...]).astype(BF16)
    q = mm(normed, w_ref[0]).astype(BF16)
    qkv_ref[0, 0] = q
    qkv_ref[0, 1] = mm(normed, w_ref[1]).astype(BF16)
    qkv_ref[0, 2] = mm(normed, w_ref[2]).astype(BF16)
    for g in range(size):

        @pl.when(step == g)
        def _(g=g):
            q_refs[g][...] = q


def head_attention(queries, parts):
    queries = queries * jnp.asarray(DH**-0.5, BF16)
    lane = lax.broadcasted_iota(jnp.int32, (1, queries.shape[0]), 1)
    blocks = []
    for keys, _, biases, firsts in parts:
        s = lax.dot_general(keys, queries, (((1,), (1,)), ((), ())), preferred_element_type=F32)
        for i, (bias, first) in enumerate(zip(biases, firsts)):
            block = s[i * STAB : (i + 1) * STAB] + bias
            if first:
                block = jnp.where(lane >= first, block, -1e30)
            blocks.append(block)
    top = blocks[0]
    for block in blocks[1:]:
        top = jnp.maximum(top, block)
    top = jnp.max(top, axis=0, keepdims=True)
    weights = [jnp.exp(block - top) for block in blocks]
    total = weights[0]
    for w in weights[1:]:
        total = total + w
    total = jnp.sum(total, axis=0, keepdims=True)
    at, summed = 0, None
    for _, values, biases, _ in parts:
        w = jnp.concatenate([x.astype(BF16) for x in weights[at : at + len(biases)]], axis=0)
        at += len(biases)
        term = lax.dot_general(values, w, (((0,), (0,)), ((), ())), preferred_element_type=F32)
        summed = term if summed is None else summed + term
    return summed / total, top + jnp.log(total)


def cache_part(cache_ref, head, age_ref, row, slope, rounds):
    kv = cache_ref[0, head]
    biases = [-slope * age_ref[row, r].astype(F32) for r in range(rounds)]
    return kv[:, :DH], kv[:, DH:], biases, [0] * rounds


def near_kernel(first, heads, rounds, new_rounds, order_ref, qkv_ref, cache_ref, age_ref, slope_ref, after_ref, o_ref):
    row = order_ref[pl.program_id(0) + first]
    hd = heads * DH
    for h in range(heads):
        cols = slice(h * DH, (h + 1) * DH)
        slope = slope_ref[h]
        fresh = (
            qkv_ref[0, 1, :, cols],
            qkv_ref[0, 2, :, cols],
            [slope * float(r) for r in range(new_rounds)],
            [r * STAB for r in range(new_rounds)],
        )
        out, lse = head_attention(qkv_ref[0, 0, :, cols], [cache_part(cache_ref, h, age_ref, row, slope, rounds), fresh])
        o_ref[0, cols, :] = out
        o_ref[0, hd + h : hd + h + 1, :] = lse


def far_kernel(first, size, heads, rounds, order_ref, *refs):
    q_refs = refs[:size]
    cache_ref, age_ref, slope_ref, _ = refs[size : size + 4]
    o_refs, (out_scr, lse_scr) = refs[size + 4 : 2 * size + 4], refs[-2:]
    step = pl.program_id(0)
    row = order_ref[first + step]
    hd = heads * DH
    lse_scr[...] = jnp.zeros_like(lse_scr)
    for h in range(heads):
        cols = slice(h * DH, (h + 1) * DH)
        q = q_refs[0][:, cols]
        for g in range(1, size):
            q = jnp.where(step == g, q_refs[g][:, cols], q)
        out, lse = head_attention(q, [cache_part(cache_ref, h, age_ref, row, slope_ref[h], rounds)])
        out_scr[cols, :] = out.astype(BF16)
        hi = lse.astype(BF16).astype(F32)
        mid = (lse - hi).astype(BF16).astype(F32)
        lse_scr[h : h + 1, :] = hi
        lse_scr[heads + h : heads + h + 1, :] = mid
        lse_scr[2 * heads + h : 2 * heads + h + 1, :] = lse - hi - mid
    out_scr[hd:, :] = lse_scr[...].astype(BF16)
    for g in range(size):

        @pl.when(step == g)
        def _(g=g):
            o_refs[g][...] = out_scr[...]


def join_kernel(size, heads, pos_ref, near_ref, *refs):
    far_refs, outs, scr = refs[:size], refs[size + 1 : -1], refs[-1]
    hd = heads * DH
    for g, far_ref in enumerate(far_refs):
        tail = far_ref[hd:, :].astype(F32)
        lse_far = tail[:heads] + tail[heads : 2 * heads] + tail[2 * heads : 3 * heads]
        lse_near = near_ref[g, hd : hd + heads, :]
        top = jnp.maximum(lse_near, lse_far)
        a, b = jnp.exp(lse_near - top), jnp.exp(lse_far - top)
        a, b = a / (a + b), b / (a + b)
        rows = []
        for h in range(heads):
            cols = slice(h * DH, (h + 1) * DH)
            rows.append(near_ref[g, cols, :] * a[h : h + 1] + far_ref[cols, :].astype(F32) * b[h : h + 1])
        scr[...] = jnp.transpose(jnp.concatenate(rows, axis=0))
        n, count = len(outs), outs[0].shape[1]
        for r, out in enumerate(outs):
            start = pl.multiple_of(lax.rem(pos_ref[0] + r, n) * count, count)
            out[g] = scr[pl.ds(start, count), :].astype(BF16)


def mlp_kernel(group, n, steps, order_ref, pos_ref, *refs):
    size = len(group)
    pieces, xs, refs = refs[:n], refs[n : n + size], refs[n + size :]
    w_os, w_ins, w_downs, gain_ref = refs[:n], refs[n : 2 * n], refs[2 * n : 3 * n], refs[3 * n]
    out_ref, hid, acc, res, sems = refs[-5:]
    rows = pieces[0].shape[1]
    step = pl.program_id(0)

    @pl.when(step == 0)
    def _():
        for g in range(size):
            h = xs[g][0].astype(F32)
            for piece, w_o in zip(pieces, w_os):
                h += mm(piece[g], w_o[...])
            acc[g * rows : (g + 1) * rows] = h
            hid[g * rows : (g + 1) * rows] = rms(h, gain_ref[...]).astype(BF16)

    x = hid[...]
    total = acc[...]
    for w_in, w_dn in zip(w_ins, w_downs):
        total += mm(jax.nn.gelu(mm(x, w_in[...])).astype(BF16), w_dn[...])
    acc[...] = total

    @pl.when(step == steps - 1)
    def _():
        res[...] = acc[...].astype(BF16).reshape(res.shape)
        copies = [
            pltpu.make_async_copy(res.at[g], out_ref.at[order_ref[c]], sems.at[g]) for g, c in enumerate(group)
        ]
        for copy in copies:
            copy.start()
        for copy in copies:
            copy.wait()


def on_device(n_dev, n, tokens, kv_cache, cache_age, partner, slope, w_qkv, w_o, attn_gain, mlp_gain, w_in, w_down):
    count, new_len, width = tokens.shape
    heads, keys = kv_cache.shape[1], kv_cache.shape[2]
    hd = heads * DH
    rounds, new_rounds = keys // STAB, new_len // STAB
    half = n_dev // 2
    me = lax.axis_index("qubit").astype(jnp.int32)
    pos = lax.axis_index("head").astype(jnp.int32)
    owner = partner // count
    colour = jnp.where(me < half, (owner - me) % half, (me - half - owner) % half)
    slots = jnp.arange(count, dtype=jnp.int32)
    order = jnp.sum(jnp.where(colour[None, :] == slots[:, None], slots[None, :], 0), axis=1).astype(jnp.int32)
    pos1 = pos[None]
    gain1, gain2 = attn_gain[None], mlp_gain[None]
    perms = []
    for c in range(count):
        pairs = [(d, half + (d + c) % half) for d in range(half)]
        perms.append(pairs + [(b, a) for a, b in pairs])
    swaps = [[(a, (a + r) % n) for a in range(n)] for r in range(n)]
    sources = [(pos - r) % n for r in range(n)]
    w_os = [lax.dynamic_slice_in_dim(w_o, src * hd, hd, 0) for src in sources]

    w_ins, w_downs = [w_in], [w_down]
    for r in range(1, n):
        w_ins.append(lax.ppermute(w_in, "head", swaps[r]))
        w_downs.append(lax.ppermute(w_down, "head", swaps[r]))

    after = order
    got_q = []
    block = jax.ShapeDtypeStruct((new_len, hd), BF16)
    qkvs, nears = [], []
    for first in range(0, count, PROJ):
        qkv, *qs = pl.pallas_call(
            functools.partial(project_kernel, PROJ),
            grid_spec=pltpu.PrefetchScalarGridSpec(
                num_scalar_prefetch=1,
                grid=(PROJ,),
                in_specs=[
                    pl.BlockSpec((1, new_len, width), lambda i, o, f=first: (o[f + i], 0, 0)),
                    whole((1, width)),
                    whole((3, width, hd)),
                    ANY_SPEC,
                ],
                out_specs=[pl.BlockSpec((1, 3, new_len, hd), lambda i, o: (i, 0, 0, 0))]
                + [whole((new_len, hd))] * PROJ,
            ),
            out_shape=[jax.ShapeDtypeStruct((PROJ, 3, new_len, hd), BF16)] + [block] * PROJ,
            compiler_params=params(),
            cost_estimate=cost(6 * PROJ * new_len * width * hd, 1500000 * PROJ),
        )(order, tokens, gain1, w_qkv, after)
        after = qkv
        qkvs.append(qkv)
        for g in range(PROJ):
            got_q.append(lax.ppermute(qs[g], "qubit", perms[first + g]))

    def cache_spec(first):
        return pl.BlockSpec((1, heads, keys, 2 * DH), lambda i, o: (o[first + i], 0, 0, 0))

    for first in range(0, count, PROJ):
        after = pl.pallas_call(
            functools.partial(near_kernel, first, heads, rounds, new_rounds),
            grid_spec=pltpu.PrefetchScalarGridSpec(
                num_scalar_prefetch=1,
                grid=(PROJ,),
                in_specs=[
                    pl.BlockSpec((1, 3, new_len, hd), lambda i, o: (i, 0, 0, 0)),
                    cache_spec(first),
                    SMEM_SPEC,
                    SMEM_SPEC,
                    ANY_SPEC,
                ],
                out_specs=pl.BlockSpec((1, hd + 8, new_len), lambda i, o: (i, 0, 0)),
            ),
            out_shape=jax.ShapeDtypeStruct((PROJ, hd + 8, new_len), F32),
            compiler_params=params(),
            cost_estimate=cost(16 * PROJ * heads * new_len * 640 * DH, 1000000 * PROJ),
        )(order, qkvs[first // PROJ], kv_cache, cache_age, slope, after)
        nears.append(after)

    back = []
    for first in range(0, count, GROUP):
        fars = pl.pallas_call(
            functools.partial(far_kernel, first, GROUP, heads, rounds),
            grid_spec=pltpu.PrefetchScalarGridSpec(
                num_scalar_prefetch=1,
                grid=(GROUP,),
                in_specs=[whole((new_len, hd))] * GROUP + [cache_spec(first), SMEM_SPEC, SMEM_SPEC, ANY_SPEC],
                out_specs=[whole((hd + 16, new_len))] * GROUP,
                scratch_shapes=[pltpu.VMEM((hd + 16, new_len), BF16), pltpu.VMEM((16, new_len), F32)],
            ),
            out_shape=[jax.ShapeDtypeStruct((hd + 16, new_len), BF16)] * GROUP,
            compiler_params=params(),
            cost_estimate=cost(16 * GROUP * heads * new_len * 384 * DH, 1000000 * GROUP),
        )(order, *got_q[first : first + GROUP], kv_cache, cache_age, slope, after)
        after = fars[0]
        for g in range(GROUP):
            back.append(lax.ppermute(fars[g], "qubit", perms[first + g]))

    rows = new_len // n

    def join(first, after):
        slot = (first % PROJ) // GROUP
        parts = pl.pallas_call(
            functools.partial(join_kernel, GROUP, heads),
            grid=(1,),
            in_specs=[SMEM_SPEC, pl.BlockSpec((GROUP, hd + 8, new_len), lambda i: (slot, 0, 0))]
            + [whole((hd + 16, new_len))] * GROUP
            + [ANY_SPEC],
            out_specs=[whole((GROUP, rows, hd))] * n,
            out_shape=[jax.ShapeDtypeStruct((GROUP, rows, hd), BF16)] * n,
            scratch_shapes=[pltpu.VMEM((new_len, hd), F32)],
            compiler_params=params(),
            cost_estimate=cost(1000000 * GROUP, 1000000 * GROUP),
        )(pos1, nears[first // PROJ], *back[first : first + GROUP], after)
        pieces = [parts[0]] + [lax.ppermute(parts[r], "head", swaps[r]) for r in range(1, n)]
        return pieces, parts[0]

    ff = w_in.shape[1]
    steps = 2
    chunk = ff // steps
    out = None

    def mlp(group, pieces, out, after):
        size = len(group)
        x_specs = [pl.BlockSpec((1, rows, width), lambda i, o, p, c=c: (o[c], p[0], 0)) for c in group]
        ins = pieces + [tokens] * size
        ins += w_os + w_ins + w_downs + [gain2, after]
        specs = [whole((size, rows, hd))] * n + x_specs + [whole((hd, width))] * n
        specs += [pl.BlockSpec((width, chunk), lambda i, o, p: (0, i))] * n
        specs += [pl.BlockSpec((chunk, width), lambda i, o, p: (i, 0))] * n + [whole((1, width)), ANY_SPEC]
        alias = {}
        if out is not None:
            alias = {len(ins) + 2: 0}
            ins.append(out)
            specs.append(ANY_SPEC)
        return pl.pallas_call(
            functools.partial(mlp_kernel, group, n, steps),
            grid_spec=pltpu.PrefetchScalarGridSpec(
                num_scalar_prefetch=2,
                grid=(steps,),
                in_specs=specs,
                out_specs=ANY_SPEC,
                scratch_shapes=[
                    pltpu.VMEM((size * rows, width), BF16),
                    pltpu.VMEM((size * rows, width), F32),
                    pltpu.VMEM((size, rows, width), BF16),
                    pltpu.SemaphoreType.DMA((size,)),
                ],
            ),
            out_shape=jax.ShapeDtypeStruct((count, rows, width), BF16),
            input_output_aliases=alias,
            compiler_params=params(),
            cost_estimate=cost(size * rows * width * (width + 2 * n * ff) * 2, 5000000),
        )(order, pos1, *ins)

    pieces, after = join(0, after)
    for first in range(0, count, GROUP):
        here = pieces
        if first + GROUP < count:
            pieces, after = join(first + GROUP, after)
        out = mlp(tuple(range(first, first + GROUP)), here, out, after)
        after = out
    return out


def solution(mesh):
    in_specs = (
        P("qubit", None, None),
        P("qubit", "head", None, None),
        P("qubit", None),
        P("qubit"),
        P("head"),
        P(None, None, "head"),
        P(),
        P(),
        P(),
        P(None, "head"),
        P("head", None),
    )
    return jax.shard_map(
        functools.partial(on_device, mesh.shape["qubit"], mesh.shape["head"]),
        mesh=mesh,
        in_specs=in_specs,
        out_specs=P("qubit", "head", None),
        check_vma=False,
    )
```
